32 devices in a mesh: pos: 8 (over y, x, core), ang: 4 (over z).
Axes of the slice: x: 2, y: 2, z: 4, core: 2. Of those that a mesh axis runs over, the one named last changes fastest.
Arguments:
- object_field: float32 [2, 32, 256, 256], P(None, None, 'pos'), may hold values from -2.5 to 2.5
- probe_wave: float32 [2, 128, 128], replicated, may hold values from -4 to 4
- intensity: float32 [4, 32, 128, 128], P('ang', 'pos'), may hold values from 0.25 to 4
- positions: int32 [32, 2], P('pos'), may hold values from 0 to 255, as said below
- shear_steps: int32 [4, 32], replicated, may hold values from -8 to 8, as said below
Outputs:
- object_new: float32 [2, 32, 256, 256], P(None, None, 'pos')
The draws below stay inside these ranges and needn't reach their ends.
Inputs may be any that keep to these rules, and one draw needn't show every extreme that they name: `positions`: row j is (column offset, row offset). With d = j // 4 and q = j mod 4: (column offset - d * 32 + 128 // 2) mod 256 lies in 0 .. 32; it is 0 for q = 0 and 32 for q = 1; the row offset lies in 0 .. 128, and is 128 for q = 0 and 0 for q = 1. For every angle a, shear_steps[a, 0] = -8 and shear_steps[a, 31] = 8.
All inputs are finite; a program needn't handle non-finite values.
Results may differ from the reference program's by a relative error of at most 0.0001.
Values sent between devices are 32-bit elements; how exact they have to be, the bound alone decides.
A program may use at most 64 MiB of HBM per device.

```python
import jax
import jax.numpy as jnp
from jax import lax

FRAME = 128
Y = 256
Z = 32
SH = 8
ITERS = 3
TX = 32
POS_DEV = 4
X = 256
POSITIONS = 32
ANGLES = 4


def draw_positions(key, part):
    slots = jnp.arange(POSITIONS, dtype=jnp.int32)
    owner = slots // POS_DEV
    within = slots % POS_DEV
    jitter = jax.random.randint(jax.random.fold_in(key, 11), (POSITIONS,), 0, TX + 1, dtype=jnp.int32)
    jitter = jnp.where(within == 0, 0, jnp.where(within == 1, TX, jitter))
    column = (owner * TX - FRAME // 2 + jitter) % X
    rowpick = jax.random.randint(jax.random.fold_in(key, 12), (POSITIONS,), 0, Y - FRAME + 1, dtype=jnp.int32)
    rowpick = jnp.where(within == 0, Y - FRAME, jnp.where(within == 1, 0, rowpick))
    return jnp.stack([column, rowpick], axis=1).astype(jnp.int32)


def draw_shear_steps(key, part):
    steps = jax.random.randint(jax.random.fold_in(key, 13), (ANGLES, Z), -SH, SH + 1, dtype=jnp.int32)
    depth = jnp.arange(Z, dtype=jnp.int32)[None, :]
    steps = jnp.where(depth == 0, -SH, jnp.where(depth == Z - 1, SH, steps))
    return steps.astype(jnp.int32)


def block_levels(own_key, dims, shards, smallest, high):
    factor_of, own = 1.0, jax.random.fold_in(own_key, 6)
    for axis_at, shards_of in shards:
        steps = jnp.exp(jax.random.uniform(jax.random.fold_in(own, axis_at), (shards_of,), jnp.float32, smallest / len(shards), high / len(shards)))
        factor_of = factor_of * jnp.repeat(steps, dims[axis_at] // shards_of).reshape([-1 if axis == axis_at else 1 for axis in range(len(dims))])
    return factor_of


def bell_draw(own_key, shape, deviation, most, split=(), kind=jnp.bfloat16):
    loudness = block_levels(own_key, shape, split, -0.22, 0.18) if split else 1.0
    drawn = jax.random.normal(own_key, shape, jnp.float32) * deviation * loudness
    return jnp.minimum(jnp.maximum(drawn, -most), most).astype(kind)


def setup_inputs(seed: int = 0) -> dict:
    seeds = jax.random.split(jax.random.key(seed), 6)
    return {
        "object_field": bell_draw(seeds[0], (2, Z, X, Y), 0.25, 2.5, ((2, 8),), jnp.float32),
        "probe_wave": bell_draw(seeds[1], (2, FRAME, FRAME), 0.7, 4.0, (), jnp.float32),
        "intensity": jnp.clip(0.25 + 3.75 * jax.random.uniform(seeds[2], (ANGLES, POSITIONS, FRAME, FRAME), jnp.float32) ** block_levels(seeds[2], (ANGLES, POSITIONS, FRAME, FRAME), ((0, 4), (1, 8)), -0.2, 0.2), 0.25, 4.0),
        "positions": draw_positions(jax.random.fold_in(seeds[5], 71), 0),
        "shear_steps": draw_shear_steps(jax.random.fold_in(seeds[5], 71), 0),
    }


MODULUS_FLOOR = 0.25
INTERSECTION_WEIGHT = 1.0
RELAXATION = 0.5

def project_object(object_field, steps):
    layers = jax.vmap(lambda layer, step: jnp.roll(layer, -step, axis=1), in_axes=(1, 0))(object_field, steps)
    return lax.optimization_barrier(jnp.sum(layers, axis=0))

def spread_back(change, steps):
    layers = jax.vmap(lambda step: jnp.roll(change, step, axis=1))(steps)
    return jnp.moveaxis(layers, 0, 1)

def reference(object_field, probe_wave, intensity, positions, shear_steps):
    offsets = jnp.arange(FRAME, dtype=jnp.int32)
    columns = ((positions[:, 0:1] + offsets[None, :]) % X)[:, :, None]
    row_index = (positions[:, 1:2] + offsets[None, :])[:, None, :]
    probe_power = probe_wave[0] * probe_wave[0] + probe_wave[1] * probe_wave[1]
    coverage = jnp.zeros((X, Y), jnp.float32).at[columns, row_index].add(jnp.broadcast_to(probe_power, (POSITIONS, FRAME, FRAME)))
    probe_complex = lax.complex(probe_wave[0], probe_wave[1])

    def one_angle(accumulated, item):
        frames, steps = item
        amplitude = jnp.sqrt(frames)
        projected = project_object(object_field, steps)
        estimate = projected
        for iteration in range(ITERS):
            patches = lax.complex(estimate[0][columns, row_index], estimate[1][columns, row_index])
            wave = jnp.fft.fft2(probe_complex * patches, norm='ortho')
            modulus = jnp.sqrt(wave.real * wave.real + wave.imag * wave.imag)
            wave = wave * (amplitude / jnp.maximum(modulus, MODULUS_FLOOR))
            back = jnp.conj(probe_complex) * jnp.fft.ifft2(wave, norm='ortho')
            numerator = jnp.zeros((2, X, Y), jnp.float32).at[:, columns, row_index].add(jnp.stack([back.real, back.imag]))
            estimate = (numerator + INTERSECTION_WEIGHT * estimate) / (coverage + INTERSECTION_WEIGHT)
        return (accumulated + spread_back(estimate - projected, steps), None)
    accumulated, unused = lax.scan(one_angle, jnp.zeros(object_field.shape, jnp.float32), (intensity, shear_steps))
    return object_field + RELAXATION / ANGLES * accumulated
```

```python
import functools

import jax
import jax.numpy as jnp
import numpy as np
from jax import lax
from jax.experimental import pallas as pl
from jax.experimental.pallas import tpu as pltpu
from jax.sharding import PartitionSpec as P

SH = 8
ITERS = 3
MODULUS_FLOOR = 0.25
INTERSECTION_WEIGHT = 1.0
RELAXATION = 0.5
MESH = pl.DeviceIdType.MESH
F32 = jnp.float32
BF16 = jnp.bfloat16


def dft_tables(length):
    index = np.arange(length)
    phases = (index[:, None] * index[None, :] % length) * (2.0 * np.pi / length)
    cosine = np.cos(phases) / np.sqrt(length)
    sine = np.sin(phases) / np.sqrt(length)
    a = np.block([[cosine, sine], [-sine, cosine]])
    parts = []
    for table in (a, a.T):
        high = table.astype(np.float32).astype(jnp.bfloat16)
        low = (table - high.astype(np.float64)).astype(np.float32).astype(jnp.bfloat16)
        parts += [high, low]
    return np.stack(parts)


def split(x):
    high = x.astype(BF16)
    return high, (x - high.astype(F32)).astype(BF16)


def dot(a, b):
    return jnp.dot(a, b, preferred_element_type=F32)


def times_right(x, high, low):
    x_high, x_low = split(x)
    return dot(x_high, high) + (dot(x_low, high) + dot(x_high, low))


def times_left(high, low, x):
    x_high, x_low = split(x)
    return dot(high, x_high) + (dot(high, x_low) + dot(low, x_high))


def update_kernel(
    n_pos, n_ang,
    positions, steps, object_hbm, probe, intensity, tables,
    gathered,
    held, rolled, amplitude, cover, cover_in, inverse, canvas, rim_in, first, source, summed, sums_in,
    load_sem, cover_send, cover_recv, rim_send, rim_recv, est_send, est_recv,
    sum_send, sum_recv, edge_send, edge_recv, core_send, core_recv, side_send, side_recv,
):
    me = lax.axis_index("pos")
    ang = lax.axis_index("ang")
    layers, tile, rows = held.shape[1], first.shape[1], first.shape[2]
    frame = probe.shape[1]
    half = rows - frame
    frames = positions.shape[0]
    bands = source.shape[1] // tile
    reach = bands // 2
    width = n_pos * tile
    offsets = [t for t in range(bands) if t != reach]

    def at(shift):
        return lax.rem(me + (shift + n_pos), n_pos)

    def peer(shift):
        return lax.rem(ang + (shift + n_ang), n_ang)

    load = pltpu.make_async_copy(object_hbm, held, load_sem)
    load.start()

    barrier = pltpu.get_barrier_semaphore()
    for t in offsets:
        pl.semaphore_signal(barrier, inc=1, device_id={"pos": at(t - reach)}, device_id_type=MESH)
    for d in range(1, n_ang):
        pl.semaphore_signal(barrier, inc=1, device_id={"ang": peer(d)}, device_id_type=MESH)

    lane = lax.broadcasted_iota(jnp.int32, (tile, frame), 1)
    row = lax.broadcasted_iota(jnp.int32, (tile, frame), 0)
    col_at = []
    row_at = []
    for j in range(frames):
        col_at.append(lax.rem(positions[j, 0] - me * tile + (reach * tile + width), width))
        row_at.append(positions[j, 1])

    def unfold(j, block, target, channel, is_first):
        low_half = lane >= row_at[j]
        low_cols = row >= col_at[j]
        zero = jnp.zeros((tile, frame), F32)

        def put(at_row, at_lane, value):
            index = (pl.ds(at_row, tile), pl.ds(at_lane, frame))
            index = index if channel is None else (channel,) + index
            if is_first:
                target[index] = value
            else:
                target[index] += value

        for t in range(bands - 1):
            piece = block[t * tile : (t + 1) * tile]
            low = jnp.where(low_half, piece, zero)
            high = jnp.where(low_half, zero, piece)
            if t == 0:
                put(0, 0, jnp.where(low_cols, low, zero))
                put(0, half, jnp.where(low_cols, high, zero))
                put((bands - 1) * tile, 0, jnp.where(low_cols, zero, low))
                put((bands - 1) * tile, half, jnp.where(low_cols, zero, high))
            else:
                put(t * tile, 0, low)
                put(t * tile, half, high)

    for j in range(frames):
        power = None
        for channel in range(2):
            value = pltpu.roll(probe[channel], col_at[j], 0)
            value = pltpu.roll(value, lax.rem(row_at[j], frame), 1)
            rolled[j, channel] = value
            power = value * value if power is None else power + value * value
        unfold(j, power, cover, None, j == 0)
        amplitude[j] = jnp.sqrt(intensity[j])

    pl.semaphore_wait(barrier, len(offsets) + n_ang - 1)

    def cover_copy(t):
        return pltpu.make_async_remote_copy(
            src_ref=cover.at[pl.ds(t * tile, tile), :], dst_ref=cover_in.at[t],
            send_sem=cover_send.at[t], recv_sem=cover_recv.at[t],
            device_id={"pos": at(t - reach)}, device_id_type=MESH)

    for t in offsets:
        cover_copy(t).start()

    wide = tile + 2 * SH
    per_block = frame // tile
    lane_wide = lax.broadcasted_iota(jnp.int32, (wide, frame), 1)
    source_col = lax.rem(lane_wide, tile)
    layer_in = lane_wide // tile
    target_col = lax.broadcasted_iota(jnp.int32, (wide, frame), 0) - SH
    blocks = []
    for begin in range(0, layers, per_block):
        shift = jnp.full((wide, frame), steps[ang, begin], jnp.int32)
        for k in range(1, per_block):
            shift = jnp.where(layer_in == k, steps[ang, begin + k], shift)
        blocks.append(jnp.where(source_col == target_col + shift, 1.0, 0.0).astype(BF16))
    pick = jnp.concatenate(blocks, axis=1)
    load.wait()
    for channel in range(2):
        high, low = split(held[channel].reshape(layers * tile, rows))
        canvas[channel] = dot(pick, high) + dot(pick, low)

    def rim_copy(side):
        begin = 0 if side == 0 else SH + tile
        return pltpu.make_async_remote_copy(
            src_ref=canvas.at[:, pl.ds(begin, SH), :], dst_ref=rim_in.at[side],
            send_sem=rim_send.at[side], recv_sem=rim_recv.at[side],
            device_id={"pos": at(-1 if side == 0 else 1)}, device_id_type=MESH)

    for side in range(2):
        rim_copy(side).start()
    mine = pl.ds(reach * tile, tile)
    for side in range(2):
        rim_copy(side).wait()
    for channel in range(2):
        low = canvas[channel, pl.ds(SH, SH), :] + rim_in[1, channel]
        middle = canvas[channel, pl.ds(2 * SH, tile - 2 * SH), :]
        high = canvas[channel, pl.ds(tile, SH), :] + rim_in[0, channel]
        value = jnp.concatenate([low, middle, high], axis=0)
        first[channel] = value
        source[channel, mine, :] = value

    def est_copy(t):
        return pltpu.make_async_remote_copy(
            src_ref=source.at[:, mine, :], dst_ref=source.at[:, pl.ds(t * tile, tile), :],
            send_sem=est_send.at[t], recv_sem=est_recv.at[t],
            device_id={"pos": at(reach - t)}, device_id_type=MESH)

    def sum_copy(t):
        return pltpu.make_async_remote_copy(
            src_ref=summed.at[:, pl.ds(t * tile, tile), :], dst_ref=sums_in.at[t],
            send_sem=sum_send.at[t], recv_sem=sum_recv.at[t],
            device_id={"pos": at(t - reach)}, device_id_type=MESH)

    def patch(j, channel):
        low_half = lane >= row_at[j]
        low_cols = row >= col_at[j]
        pieces = []
        for t in range(bands):
            cols = pl.ds(t * tile, tile)
            pieces.append(jnp.where(
                low_half, source[channel, cols, pl.ds(0, frame)], source[channel, cols, pl.ds(half, frame)]))
        pieces[0] = jnp.where(low_cols, pieces[0], pieces[-1])
        return jnp.concatenate(pieces[:-1], axis=0)

    def transform_pair(pair):
        a_high, a_low, b_high, b_low = tables[0], tables[1], tables[2], tables[3]
        stacked = []
        for j in pair:
            real, imag = patch(j, 0), patch(j, 1)
            p_real, p_imag = rolled[j, 0], rolled[j, 1]
            stacked.append(jnp.concatenate(
                [p_real * real - p_imag * imag, p_real * imag + p_imag * real], axis=1))
        out = times_right(jnp.concatenate(stacked, axis=0), b_high, b_low)
        columns = []
        for k in range(len(pair)):
            block = out[k * frame : (k + 1) * frame]
            columns.append(jnp.concatenate([block[:, :frame], block[:, frame:]], axis=0))
        wave = times_left(a_high, a_low, jnp.concatenate(columns, axis=1))
        real, imag = wave[:frame], wave[frame:]
        amp = jnp.concatenate([amplitude[j] for j in pair], axis=1)
        factor = amp * jnp.minimum(lax.rsqrt(real * real + imag * imag), 1.0 / MODULUS_FLOOR)
        back = times_left(b_high, b_low, jnp.concatenate([real * factor, imag * factor], axis=0))
        stacked = []
        for k in range(len(pair)):
            block = back[:, k * frame : (k + 1) * frame]
            stacked.append(jnp.concatenate([block[:frame], block[frame:]], axis=1))
        return times_right(jnp.concatenate(stacked, axis=0), a_high, a_low)

    def iterate(iteration, carry):
        for t in offsets:
            est_copy(t).start()

        @pl.when(iteration == 0)
        def _():
            for t in offsets:
                cover_copy(t).wait()
            total = cover[mine, :]
            for t in offsets:
                total = total + cover_in[t]
            inverse[...] = 1.0 / (total + INTERSECTION_WEIGHT)

        for t in offsets:
            est_copy(t).wait()
        step = 2 if frames % 2 == 0 else 1
        for begin in range(0, frames, step):
            pair = list(range(begin, begin + step))
            out = transform_pair(pair)
            for k, j in enumerate(pair):
                block = out[k * frame : (k + 1) * frame]
                real, imag = block[:, :frame], block[:, frame:]
                p_real, p_imag = rolled[j, 0], rolled[j, 1]
                unfold(j, p_real * real + p_imag * imag, summed, 0, j == 0)
                unfold(j, p_real * imag - p_imag * real, summed, 1, j == 0)
        for t in offsets:
            sum_copy(t).start()
        for t in offsets:
            sum_copy(t).wait()
        for channel in range(2):
            total = summed[channel, mine, :]
            for t in offsets:
                total = total + sums_in[t, channel]
            old = source[channel, mine, :]
            source[channel, mine, :] = (total + INTERSECTION_WEIGHT * old) * inverse[...]
        return carry

    lax.fori_loop(0, ITERS, iterate, 0)

    for channel in range(2):
        gathered[ang, channel, pl.ds(SH, tile), :] = source[channel, mine, :] - first[channel]

    def edge_copy(side):
        begin, end = (SH, SH + tile) if side == 0 else (tile, 0)
        return pltpu.make_async_remote_copy(
            src_ref=gathered.at[ang, :, pl.ds(begin, SH), :], dst_ref=gathered.at[ang, :, pl.ds(end, SH), :],
            send_sem=edge_send.at[side], recv_sem=edge_recv.at[side],
            device_id={"pos": at(-1 if side == 0 else 1)}, device_id_type=MESH)

    def core_copy(d, slot):
        part = gathered.at[slot, :, pl.ds(SH, tile), :]
        return pltpu.make_async_remote_copy(
            src_ref=part, dst_ref=part, send_sem=core_send.at[d], recv_sem=core_recv.at[d],
            device_id={"ang": peer(d)}, device_id_type=MESH)

    def side_copy(d, side, slot):
        part = gathered.at[slot, :, pl.ds(0 if side == 0 else SH + tile, SH), :]
        return pltpu.make_async_remote_copy(
            src_ref=part, dst_ref=part, send_sem=side_send.at[d, side], recv_sem=side_recv.at[d, side],
            device_id={"ang": peer(d)}, device_id_type=MESH)

    for side in range(2):
        edge_copy(side).start()
    for d in range(1, n_ang):
        core_copy(d, ang).start()
    for side in range(2):
        edge_copy(side).wait()
    for d in range(1, n_ang):
        for side in range(2):
            side_copy(d, side, ang).start()
    for d in range(1, n_ang):
        core_copy(d, ang).wait_send()
        core_copy(d, peer(-d)).wait_recv()
        for side in range(2):
            side_copy(d, side, ang).wait_send()
            side_copy(d, side, peer(-d)).wait_recv()


def spread_kernel(weight, steps, object_block, gathered, out):
    _, depth, tile, rows = object_block.shape
    n_ang, _, wide, _ = gathered.shape
    first_layer = pl.program_id(0) * depth
    lane = lax.broadcasted_iota(jnp.int32, (tile, n_ang * wide), 1)
    offset = lane - lax.broadcasted_iota(jnp.int32, (tile, n_ang * wide), 0)
    blocks = []
    for z in range(depth):
        chosen = None
        for a in range(n_ang):
            begin = a * wide
            inside = (lane >= begin) & (lane < begin + wide)
            hit = inside & (offset == begin + SH - steps[a, first_layer + z])
            chosen = hit if chosen is None else chosen | hit
        blocks.append(jnp.where(chosen, 1.0, 0.0))
    pick = jnp.concatenate(blocks, axis=0).astype(BF16)
    for channel in range(2):
        high, low = split(gathered[:, channel].reshape(n_ang * wide, rows))
        total = dot(pick, high) + dot(pick, low)
        out[channel] = object_block[channel] + weight * total.reshape(depth, tile, rows)


def per_device(n_pos, n_ang, object_field, probe_wave, intensity, positions, shear_steps):
    _, layers, tile, rows = object_field.shape
    frame = probe_wave.shape[1]
    frames = positions.shape[0]
    reach = -(-(frame // 2) // tile)
    bands = 2 * reach + 1
    assert intensity.shape[0] == 1 and frame == 2 * reach * tile and rows == 2 * frame
    assert n_pos >= bands
    tables = jnp.asarray(dft_tables(frame))
    wide = tile + 2 * SH
    vmem = pl.BlockSpec(memory_space=pltpu.VMEM)
    smem = pl.BlockSpec(memory_space=pltpu.SMEM)
    dma = pltpu.SemaphoreType.DMA
    gathered = pl.pallas_call(
        functools.partial(update_kernel, n_pos, n_ang),
        out_shape=jax.ShapeDtypeStruct((n_ang, 2, wide, rows), F32),
        in_specs=[smem, smem, pl.BlockSpec(memory_space=pl.ANY), vmem, vmem, vmem],
        out_specs=vmem,
        scratch_shapes=[
            pltpu.VMEM((2, layers, tile, rows), F32),
            pltpu.VMEM((frames, 2, frame, frame), F32),
            pltpu.VMEM((frames, frame, frame), F32),
            pltpu.VMEM((bands * tile, rows), F32),
            pltpu.VMEM((bands, tile, rows), F32),
            pltpu.VMEM((tile, rows), F32),
            pltpu.VMEM((2, wide, rows), F32),
            pltpu.VMEM((2, 2, SH, rows), F32),
            pltpu.VMEM((2, tile, rows), F32),
            pltpu.VMEM((2, bands * tile, rows), F32),
            pltpu.VMEM((2, bands * tile, rows), F32),
            pltpu.VMEM((bands, 2, tile, rows), F32),
            dma,
            dma((bands,)), dma((bands,)), dma((2,)), dma((2,)), dma((bands,)), dma((bands,)),
            dma((bands,)), dma((bands,)), dma((2,)), dma((2,)), dma((n_ang,)), dma((n_ang,)),
            dma((n_ang, 2)), dma((n_ang, 2)),
        ],
        compiler_params=pltpu.CompilerParams(collective_id=0, has_side_effects=True),
        name="update",
    )(positions, shear_steps, object_field, probe_wave, intensity[0], tables)

    depth = 8 if layers % 8 == 0 else layers
    block = pl.BlockSpec((2, depth, tile, rows), lambda i: (0, i, 0, 0))
    return pl.pallas_call(
        functools.partial(spread_kernel, RELAXATION / shear_steps.shape[0]),
        out_shape=jax.ShapeDtypeStruct(object_field.shape, F32),
        grid=(layers // depth,),
        in_specs=[smem, block, vmem],
        out_specs=block,
        name="spread",
    )(shear_steps, object_field, gathered)


def solution(mesh):
    placed = (P(None, None, "pos", None), P(), P("ang", "pos", None, None), P("pos", None), P())
    return jax.shard_map(
        functools.partial(per_device, mesh.shape["pos"], mesh.shape["ang"]),
        mesh=mesh,
        in_specs=placed,
        out_specs=P(None, None, "pos", None),
        check_vma=False,
    )
```

```python
import functools

import jax
import jax.numpy as jnp
import numpy as np
from jax import lax
from jax.experimental import pallas as pl
from jax.experimental.pallas import tpu as pltpu
from jax.sharding import PartitionSpec as P

SH = 8
ITERS = 3
MODULUS_FLOOR = 0.25
INTERSECTION_WEIGHT = 1.0
RELAXATION = 0.5
MESH = pl.DeviceIdType.MESH
F32 = jnp.float32
BF16 = jnp.bfloat16


def dft_tables(length):
    index = np.arange(length)
    phases = (index[:, None] * index[None, :] % length) * (2.0 * np.pi / length)
    cosine = np.cos(phases) / np.sqrt(length)
    sine = np.sin(phases) / np.sqrt(length)
    a = np.block([[cosine, sine], [-sine, cosine]])
    parts = []
    for table in (a, a.T):
        high = table.astype(np.float32).astype(jnp.bfloat16)
        low = (table - high.astype(np.float64)).astype(np.float32).astype(jnp.bfloat16)
        parts += [high, low]
    return np.stack(parts)


def split(x):
    high = x.astype(BF16)
    return high, (x - high.astype(F32)).astype(BF16)


def dot(a, b):
    return jnp.dot(a, b, preferred_element_type=F32)


def times_right(x, high, low):
    x_high, x_low = split(x)
    return dot(x_high, high) + (dot(x_low, high) + dot(x_high, low))


def times_left(high, low, x):
    x_high, x_low = split(x)
    return dot(high, x_high) + (dot(high, x_low) + dot(low, x_high))


def update_kernel(
    n_pos, n_ang,
    positions, steps, object_hbm, probe, intensity, tables,
    gathered,
    held, rolled, amplitude, cover, cover_in, inverse, canvas, rim_in, first, source, summed, sums_in, waves,
    load_sem, cover_send, cover_recv, rim_send, rim_recv, est_send, est_recv,
    sum_send, sum_recv, edge_send, edge_recv, core_send, core_recv, side_send, side_recv,
):
    me = lax.axis_index("pos")
    ang = lax.axis_index("ang")
    layers, tile, rows = held.shape[1], first.shape[1], first.shape[2]
    frame = probe.shape[1]
    half = rows - frame
    frames = positions.shape[1]
    bands = source.shape[1] // tile
    reach = bands // 2
    width = n_pos * tile
    offsets = [t for t in range(bands) if t != reach]

    def at(shift):
        return lax.rem(me + (shift + n_pos), n_pos)

    def peer(shift):
        return lax.rem(ang + (shift + n_ang), n_ang)

    load = pltpu.make_async_copy(object_hbm, held, load_sem)
    load.start()

    barrier = pltpu.get_barrier_semaphore()
    for t in offsets:
        pl.semaphore_signal(barrier, inc=1, device_id={"pos": at(t - reach)}, device_id_type=MESH)
    for d in range(1, n_ang):
        pl.semaphore_signal(barrier, inc=1, device_id={"ang": peer(d)}, device_id_type=MESH)

    lane = lax.broadcasted_iota(jnp.int32, (tile, frame), 1)
    row = lax.broadcasted_iota(jnp.int32, (tile, frame), 0)
    col_at = []
    row_at = []
    for j in range(frames):
        col_at.append(lax.rem(positions[0, j] - me * tile + (reach * tile + width), width))
        row_at.append(positions[1, j])

    def unfold(t, pieces):
        sums = [[None, None], [None, None]] if t == 0 else [[None, None]]
        zero = jnp.zeros((tile, frame), F32)
        for j, piece in enumerate(pieces):
            low_half = lane >= row_at[j]
            parts = [jnp.where(low_half, piece, zero), jnp.where(low_half, zero, piece)]
            for lanes in range(2):
                values = [parts[lanes]]
                if t == 0:
                    low_cols = row >= col_at[j]
                    values = [jnp.where(low_cols, parts[lanes], zero), jnp.where(low_cols, zero, parts[lanes])]
                for place, value in enumerate(values):
                    old = sums[place][lanes]
                    sums[place][lanes] = value if old is None else old + value
        targets = [t, bands - 1] if t == 0 else [t]
        return [(target, jnp.concatenate(sums[place], axis=1)) for place, target in enumerate(targets)]

    wide = tile + 2 * SH
    per_block = frame // tile
    lane_wide = lax.broadcasted_iota(jnp.int32, (wide, frame), 1)
    source_col = lax.rem(lane_wide, tile)
    layer_in = lane_wide // tile
    target_col = lax.broadcasted_iota(jnp.int32, (wide, frame), 0) - SH
    blocks = []
    for begin in range(0, layers, per_block):
        shift = jnp.full((wide, frame), steps[ang, begin], jnp.int32)
        for k in range(1, per_block):
            shift = jnp.where(layer_in == k, steps[ang, begin + k], shift)
        blocks.append(jnp.where(source_col == target_col + shift, 1.0, 0.0).astype(BF16))
    pick = jnp.concatenate(blocks, axis=1)
    load.wait()
    for channel in range(2):
        high, low = split(held[channel].reshape(layers * tile, rows))
        canvas[channel] = dot(pick, high) + dot(pick, low)

    pl.semaphore_wait(barrier, len(offsets) + n_ang - 1)

    def rim_copy(side):
        begin = 0 if side == 0 else SH + tile
        return pltpu.make_async_remote_copy(
            src_ref=canvas.at[:, pl.ds(begin, SH), :], dst_ref=rim_in.at[side],
            send_sem=rim_send.at[side], recv_sem=rim_recv.at[side],
            device_id={"pos": at(-1 if side == 0 else 1)}, device_id_type=MESH)

    for side in range(2):
        rim_copy(side).start()
    for j in range(frames):
        for channel in range(2):
            value = pltpu.roll(probe[channel], col_at[j], 0)
            rolled[j, channel] = pltpu.roll(value, lax.rem(row_at[j], frame), 1)
        amplitude[:, pl.ds(j * frame, frame)] = jnp.sqrt(intensity[j])
    for t in range(bands - 1):
        cols = pl.ds(t * tile, tile)
        powers = [rolled[j, 0, cols, :] ** 2 + rolled[j, 1, cols, :] ** 2 for j in range(frames)]
        for target, value in unfold(t, powers):
            cover[pl.ds(target * tile, tile), :] = value

    def cover_copy(t):
        return pltpu.make_async_remote_copy(
            src_ref=cover.at[pl.ds(t * tile, tile), :], dst_ref=cover_in.at[t],
            send_sem=cover_send.at[t], recv_sem=cover_recv.at[t],
            device_id={"pos": at(t - reach)}, device_id_type=MESH)

    mine = pl.ds(reach * tile, tile)
    for side in range(2):
        rim_copy(side).wait()
    for channel in range(2):
        low = canvas[channel, pl.ds(SH, SH), :] + rim_in[1, channel]
        middle = canvas[channel, pl.ds(2 * SH, tile - 2 * SH), :]
        high = canvas[channel, pl.ds(tile, SH), :] + rim_in[0, channel]
        value = jnp.concatenate([low, middle, high], axis=0)
        first[channel] = value
        source[channel, mine, :] = value

    def est_copy(t):
        return pltpu.make_async_remote_copy(
            src_ref=source.at[:, mine, :], dst_ref=source.at[:, pl.ds(t * tile, tile), :],
            send_sem=est_send.at[t], recv_sem=est_recv.at[t],
            device_id={"pos": at(reach - t)}, device_id_type=MESH)

    def sum_copy(t):
        return pltpu.make_async_remote_copy(
            src_ref=summed.at[:, pl.ds(t * tile, tile), :], dst_ref=sums_in.at[t],
            send_sem=sum_send.at[t], recv_sem=sum_recv.at[t],
            device_id={"pos": at(t - reach)}, device_id_type=MESH)

    def fold(t, channel, j):
        low_half = lane >= row_at[j]

        def columns(at_tile):
            cols = pl.ds(at_tile * tile, tile)
            return jnp.where(
                low_half, source[channel, cols, pl.ds(0, frame)], source[channel, cols, pl.ds(half, frame)])

        if t > 0:
            return columns(t)
        return jnp.where(row >= col_at[j], columns(0), columns(bands - 1))

    def forward_rows(t):
        cols = pl.ds(t * tile, tile)
        stacked = []
        for j in range(frames):
            real, imag = fold(t, 0, j), fold(t, 1, j)
            p_real, p_imag = rolled[j, 0, cols, :], rolled[j, 1, cols, :]
            stacked.append(jnp.concatenate(
                [p_real * real - p_imag * imag, p_real * imag + p_imag * real], axis=1))
        out = times_right(jnp.concatenate(stacked, axis=0), tables[2], tables[3])
        for j in range(frames):
            block = out[j * tile : (j + 1) * tile]
            lanes = pl.ds(j * frame, frame)
            waves[cols, lanes] = block[:, :frame]
            waves[pl.ds(frame + t * tile, tile), lanes] = block[:, frame:]

    def correct(begin, count):
        lanes = pl.ds(begin * frame, count * frame)
        wave = times_left(tables[0], tables[1], waves[:, lanes])
        real, imag = wave[:frame], wave[frame:]
        factor = amplitude[:, lanes] * jnp.minimum(
            lax.rsqrt(real * real + imag * imag), 1.0 / MODULUS_FLOOR)
        waves[:, lanes] = times_left(
            tables[2], tables[3], jnp.concatenate([real * factor, imag * factor], axis=0))

    def backward_rows(t):
        cols = pl.ds(t * tile, tile)
        stacked = []
        for j in range(frames):
            lanes = pl.ds(j * frame, frame)
            stacked.append(jnp.concatenate(
                [waves[cols, lanes], waves[pl.ds(frame + t * tile, tile), lanes]], axis=1))
        out = times_right(jnp.concatenate(stacked, axis=0), tables[0], tables[1])
        back_real, back_imag = [], []
        for j in range(frames):
            block = out[j * tile : (j + 1) * tile]
            real, imag = block[:, :frame], block[:, frame:]
            p_real, p_imag = rolled[j, 0, cols, :], rolled[j, 1, cols, :]
            back_real.append(p_real * real + p_imag * imag)
            back_imag.append(p_real * imag - p_imag * real)
        for channel, pieces in enumerate((back_real, back_imag)):
            for target, value in unfold(t, pieces):
                summed[channel, pl.ds(target * tile, tile), :] = value

    order = sorted(range(1, bands - 1), key=lambda t: -abs(t - reach))

    def iterate(iteration, carry):
        for t in offsets:
            est_copy(t).start()
        for t in reversed(order):
            if t != reach:
                est_copy(t).wait()
            forward_rows(t)
        for t in (0, bands - 1):
            est_copy(t).wait()

        @pl.when(iteration == 0)
        def _():
            for t in offsets:
                cover_copy(t).start()

        forward_rows(0)
        step = 2 if frames % 2 == 0 else 1
        for begin in range(0, frames, step):
            correct(begin, step)
        backward_rows(0)
        for t in (0, bands - 1):
            sum_copy(t).start()
        for t in order:
            backward_rows(t)
            if t != reach:
                sum_copy(t).start()

        @pl.when(iteration == 0)
        def _():
            for t in offsets:
                cover_copy(t).wait()
            total = cover[mine, :]
            for t in offsets:
                total = total + cover_in[t]
            inverse[...] = 1.0 / (total + INTERSECTION_WEIGHT)

        for t in offsets:
            sum_copy(t).wait()
        for channel in range(2):
            total = summed[channel, mine, :]
            for t in offsets:
                total = total + sums_in[t, channel]
            old = source[channel, mine, :]
            source[channel, mine, :] = (total + INTERSECTION_WEIGHT * old) * inverse[...]
        return carry

    lax.fori_loop(0, ITERS, iterate, 0)

    for channel in range(2):
        gathered[ang, channel, pl.ds(SH, tile), :] = source[channel, mine, :] - first[channel]

    def edge_copy(side):
        begin, end = (SH, SH + tile) if side == 0 else (tile, 0)
        return pltpu.make_async_remote_copy(
            src_ref=gathered.at[ang, :, pl.ds(begin, SH), :], dst_ref=gathered.at[ang, :, pl.ds(end, SH), :],
            send_sem=edge_send.at[side], recv_sem=edge_recv.at[side],
            device_id={"pos": at(-1 if side == 0 else 1)}, device_id_type=MESH)

    def core_copy(d, slot):
        part = gathered.at[slot, :, pl.ds(SH, tile), :]
        return pltpu.make_async_remote_copy(
            src_ref=part, dst_ref=part, send_sem=core_send.at[d], recv_sem=core_recv.at[d],
            device_id={"ang": peer(d)}, device_id_type=MESH)

    def side_copy(d, side, slot):
        part = gathered.at[slot, :, pl.ds(0 if side == 0 else SH + tile, SH), :]
        return pltpu.make_async_remote_copy(
            src_ref=part, dst_ref=part, send_sem=side_send.at[d, side], recv_sem=side_recv.at[d, side],
            device_id={"ang": peer(d)}, device_id_type=MESH)

    for side in range(2):
        edge_copy(side).start()
    for d in range(1, n_ang):
        core_copy(d, ang).start()
    for side in range(2):
        edge_copy(side).wait()
    for d in range(1, n_ang):
        for side in range(2):
            side_copy(d, side, ang).start()
    for d in range(1, n_ang):
        core_copy(d, ang).wait_send()
        core_copy(d, peer(-d)).wait_recv()
        for side in range(2):
            side_copy(d, side, ang).wait_send()
            side_copy(d, side, peer(-d)).wait_recv()


def spread_kernel(weight, steps, object_block, gathered, out):
    _, depth, tile, rows = object_block.shape
    n_ang, _, wide, _ = gathered.shape
    first_layer = pl.program_id(0) * depth
    lane = lax.broadcasted_iota(jnp.int32, (tile, n_ang * wide), 1)
    offset = lane - lax.broadcasted_iota(jnp.int32, (tile, n_ang * wide), 0)
    blocks = []
    for z in range(depth):
        chosen = None
        for a in range(n_ang):
            begin = a * wide
            inside = (lane >= begin) & (lane < begin + wide)
            hit = inside & (offset == begin + SH - steps[a, first_layer + z])
            chosen = hit if chosen is None else chosen | hit
        blocks.append(jnp.where(chosen, 1.0, 0.0))
    pick = jnp.concatenate(blocks, axis=0).astype(BF16)
    for channel in range(2):
        high, low = split(gathered[:, channel].reshape(n_ang * wide, rows))
        total = dot(pick, high) + dot(pick, low)
        out[channel] = object_block[channel] + weight * total.reshape(depth, tile, rows)


def per_device(n_pos, n_ang, object_field, probe_wave, intensity, positions, shear_steps):
    _, layers, tile, rows = object_field.shape
    frame = probe_wave.shape[1]
    frames = positions.shape[0]
    reach = -(-(frame // 2) // tile)
    bands = 2 * reach + 1
    assert intensity.shape[0] == 1 and frame == 2 * reach * tile and rows == 2 * frame
    assert n_pos >= bands
    tables = jnp.asarray(dft_tables(frame))
    wide = tile + 2 * SH
    vmem = pl.BlockSpec(memory_space=pltpu.VMEM)
    smem = pl.BlockSpec(memory_space=pltpu.SMEM)
    dma = pltpu.SemaphoreType.DMA
    gathered = pl.pallas_call(
        functools.partial(update_kernel, n_pos, n_ang),
        out_shape=jax.ShapeDtypeStruct((n_ang, 2, wide, rows), F32),
        in_specs=[smem, smem, pl.BlockSpec(memory_space=pl.ANY), vmem, vmem, vmem],
        out_specs=vmem,
        scratch_shapes=[
            pltpu.VMEM((2, layers, tile, rows), F32),
            pltpu.VMEM((frames, 2, frame, frame), F32),
            pltpu.VMEM((frame, frames * frame), F32),
            pltpu.VMEM((bands * tile, rows), F32),
            pltpu.VMEM((bands, tile, rows), F32),
            pltpu.VMEM((tile, rows), F32),
            pltpu.VMEM((2, wide, rows), F32),
            pltpu.VMEM((2, 2, SH, rows), F32),
            pltpu.VMEM((2, tile, rows), F32),
            pltpu.VMEM((2, bands * tile, rows), F32),
            pltpu.VMEM((2, bands * tile, rows), F32),
            pltpu.VMEM((bands, 2, tile, rows), F32),
            pltpu.VMEM((2 * frame, frames * frame), F32),
            dma,
            dma((bands,)), dma((bands,)), dma((2,)), dma((2,)), dma((bands,)), dma((bands,)),
            dma((bands,)), dma((bands,)), dma((2,)), dma((2,)), dma((n_ang,)), dma((n_ang,)),
            dma((n_ang, 2)), dma((n_ang, 2)),
        ],
        compiler_params=pltpu.CompilerParams(collective_id=0, has_side_effects=True),
        name="update",
    )(positions.T, shear_steps, object_field, probe_wave, intensity[0], tables)

    depth = 8 if layers % 8 == 0 else layers
    block = pl.BlockSpec((2, depth, tile, rows), lambda i: (0, i, 0, 0))
    return pl.pallas_call(
        functools.partial(spread_kernel, RELAXATION / shear_steps.shape[0]),
        out_shape=jax.ShapeDtypeStruct(object_field.shape, F32),
        grid=(layers // depth,),
        in_specs=[smem, block, vmem],
        out_specs=block,
        name="spread",
    )(shear_steps, object_field, gathered)


def solution(mesh):
    placed = (P(None, None, "pos", None), P(), P("ang", "pos", None, None), P("pos", None), P())
    return jax.shard_map(
        functools.partial(per_device, mesh.shape["pos"], mesh.shape["ang"]),
        mesh=mesh,
        in_specs=placed,
        out_specs=P(None, None, "pos", None),
        check_vma=False,
    )
```

```python
import functools

import jax
import jax.numpy as jnp
import numpy as np
from jax import lax
from jax.experimental import pallas as pl
from jax.experimental.pallas import tpu as pltpu
from jax.sharding import PartitionSpec as P

SH = 8
ITERS = 3
MODULUS_FLOOR = 0.25
INTERSECTION_WEIGHT = 1.0
RELAXATION = 0.5
MESH = pl.DeviceIdType.MESH
F32 = jnp.float32
BF16 = jnp.bfloat16
OUT, PAIR, FAR, EXTRA = range(4)


def dft_tables(length):
    index = np.arange(length)
    phases = (index[:, None] * index[None, :] % length) * (2.0 * np.pi / length)
    cosine = np.cos(phases) / np.sqrt(length)
    sine = np.sin(phases) / np.sqrt(length)
    a = np.block([[cosine, sine], [-sine, cosine]])
    parts = []
    for table in (a, a.T):
        high = table.astype(np.float32).astype(jnp.bfloat16)
        low = (table - high.astype(np.float64)).astype(np.float32).astype(jnp.bfloat16)
        parts += [high, low]
    return np.stack(parts)


def split(x):
    high = x.astype(BF16)
    return high, (x - high.astype(F32)).astype(BF16)


def dot(a, b):
    return jnp.dot(a, b, preferred_element_type=F32)


def times_right(x, high, low):
    x_high, x_low = split(x)
    return dot(x_high, high) + (dot(x_low, high) + dot(x_high, low))


def times_left(high, low, x):
    x_high, x_low = split(x)
    return dot(high, x_high) + (dot(high, x_low) + dot(low, x_high))


def update_kernel(
    n_pos, n_ang,
    positions, steps, object_hbm, probe, intensity, tables,
    gathered,
    held, rolled, amplitude, cover, cover_in, inverse, canvas, rim_in, first, source, summed, sums_in, waves,
    load_sem, cover_send, cover_recv, rim_send, rim_recv, est_send, est_recv,
    sum_send, sum_recv, edge_send, edge_recv, core_send, core_recv, side_send, side_recv,
):
    me = lax.axis_index("pos")
    ang = lax.axis_index("ang")
    layers, tile, rows = held.shape[1], first.shape[1], first.shape[2]
    frame = probe.shape[1]
    half = rows - frame
    frames = positions.shape[1]
    bands = source.shape[1] // tile
    reach = bands // 2
    width = n_pos * tile
    offsets = [t for t in range(bands) if t != reach]

    def at(shift):
        return lax.rem(me + (shift + n_pos), n_pos)

    def peer(shift):
        return lax.rem(ang + (shift + n_ang), n_ang)

    load = pltpu.make_async_copy(object_hbm, held, load_sem)
    load.start()

    barrier = pltpu.get_barrier_semaphore()
    for t in offsets:
        pl.semaphore_signal(barrier, inc=1, device_id={"pos": at(t - reach)}, device_id_type=MESH)
    for d in range(1, n_ang):
        pl.semaphore_signal(barrier, inc=1, device_id={"ang": peer(d)}, device_id_type=MESH)

    lane = lax.broadcasted_iota(jnp.int32, (tile, frame), 1)
    row = lax.broadcasted_iota(jnp.int32, (tile, frame), 0)
    col_at = []
    row_at = []
    for j in range(frames):
        col_at.append(lax.rem(positions[0, j] - me * tile + (reach * tile + width), width))
        row_at.append(positions[1, j])

    def unfold(t, pieces):
        sums = [[None, None], [None, None]] if t == 0 else [[None, None]]
        zero = jnp.zeros((tile, frame), F32)
        for j, piece in enumerate(pieces):
            low_half = lane >= row_at[j]
            parts = [jnp.where(low_half, piece, zero), jnp.where(low_half, zero, piece)]
            for lanes in range(2):
                values = [parts[lanes]]
                if t == 0:
                    low_cols = row >= col_at[j]
                    values = [jnp.where(low_cols, parts[lanes], zero), jnp.where(low_cols, zero, parts[lanes])]
                for place, value in enumerate(values):
                    old = sums[place][lanes]
                    sums[place][lanes] = value if old is None else old + value
        targets = [t, bands - 1] if t == 0 else [t]
        return [(target, jnp.concatenate(sums[place], axis=1)) for place, target in enumerate(targets)]

    wide = tile + 2 * SH
    per_block = frame // tile
    lane_wide = lax.broadcasted_iota(jnp.int32, (wide, frame), 1)
    source_col = lax.rem(lane_wide, tile)
    layer_in = lane_wide // tile
    target_col = lax.broadcasted_iota(jnp.int32, (wide, frame), 0) - SH
    blocks = []
    for begin in range(0, layers, per_block):
        shift = jnp.full((wide, frame), steps[ang, begin], jnp.int32)
        for k in range(1, per_block):
            shift = jnp.where(layer_in == k, steps[ang, begin + k], shift)
        blocks.append(jnp.where(source_col == target_col + shift, 1.0, 0.0).astype(BF16))
    pick = jnp.concatenate(blocks, axis=1)
    load.wait()
    for channel in range(2):
        high, low = split(held[channel].reshape(layers * tile, rows))
        canvas[channel] = dot(pick, high) + dot(pick, low)

    pl.semaphore_wait(barrier, len(offsets) + n_ang - 1)

    def rim_copy(side):
        begin = 0 if side == 0 else SH + tile
        return pltpu.make_async_remote_copy(
            src_ref=canvas.at[:, pl.ds(begin, SH), :], dst_ref=rim_in.at[side],
            send_sem=rim_send.at[side], recv_sem=rim_recv.at[side],
            device_id={"pos": at(-1 if side == 0 else 1)}, device_id_type=MESH)

    for side in range(2):
        rim_copy(side).start()
    for j in range(frames):
        for channel in range(2):
            value = pltpu.roll(probe[channel], col_at[j], 0)
            rolled[j, channel] = pltpu.roll(value, lax.rem(row_at[j], frame), 1)
        amplitude[:, pl.ds(j * frame, frame)] = jnp.sqrt(intensity[j])
    for t in range(bands - 1):
        cols = pl.ds(t * tile, tile)
        powers = [rolled[j, 0, cols, :] ** 2 + rolled[j, 1, cols, :] ** 2 for j in range(frames)]
        for target, value in unfold(t, powers):
            cover[pl.ds(target * tile, tile), :] = value

    def cover_copy(t):
        return pltpu.make_async_remote_copy(
            src_ref=cover.at[pl.ds(t * tile, tile), :], dst_ref=cover_in.at[t],
            send_sem=cover_send.at[t], recv_sem=cover_recv.at[t],
            device_id={"pos": at(t - reach)}, device_id_type=MESH)

    mine = pl.ds(reach * tile, tile)
    for side in range(2):
        rim_copy(side).wait()
    for channel in range(2):
        low = canvas[channel, pl.ds(SH, SH), :] + rim_in[1, channel]
        middle = canvas[channel, pl.ds(2 * SH, tile - 2 * SH), :]
        high = canvas[channel, pl.ds(tile, SH), :] + rim_in[0, channel]
        value = jnp.concatenate([low, middle, high], axis=0)
        first[channel] = value
        source[channel, mine, :] = value

    out_sign = 2 * lax.rem(me, 2) - 1

    def tile_at(step):
        return pl.ds(pl.multiple_of((reach + step * out_sign) * tile, tile), tile)

    def est_copy(role):
        sent, to, landing = (
            (0, 1, -1), (0, -1, 1), (0, -2, 2), (1, -1, 2))[role]
        return pltpu.make_async_remote_copy(
            src_ref=source.at[:, tile_at(sent), :], dst_ref=source.at[:, tile_at(landing), :],
            send_sem=est_send.at[role], recv_sem=est_recv.at[role],
            device_id={"pos": at(to * out_sign)}, device_id_type=MESH)

    def sum_copy(role):
        sent, to = ((1, 1), (-1, -1), (2, 2), (-2, -1))[role]
        return pltpu.make_async_remote_copy(
            src_ref=summed.at[:, tile_at(sent), :], dst_ref=sums_in.at[role],
            send_sem=sum_send.at[role], recv_sem=sum_recv.at[role],
            device_id={"pos": at(to * out_sign)}, device_id_type=MESH)

    def fold(t, channel, j):
        low_half = lane >= row_at[j]

        def columns(at_tile):
            cols = pl.ds(at_tile * tile, tile)
            return jnp.where(
                low_half, source[channel, cols, pl.ds(0, frame)], source[channel, cols, pl.ds(half, frame)])

        if t > 0:
            return columns(t)
        return jnp.where(row >= col_at[j], columns(0), columns(bands - 1))

    def forward_rows(t):
        cols = pl.ds(t * tile, tile)
        stacked = []
        for j in range(frames):
            real, imag = fold(t, 0, j), fold(t, 1, j)
            p_real, p_imag = rolled[j, 0, cols, :], rolled[j, 1, cols, :]
            stacked.append(jnp.concatenate(
                [p_real * real - p_imag * imag, p_real * imag + p_imag * real], axis=1))
        out = times_right(jnp.concatenate(stacked, axis=0), tables[2], tables[3])
        for j in range(frames):
            block = out[j * tile : (j + 1) * tile]
            lanes = pl.ds(j * frame, frame)
            waves[cols, lanes] = block[:, :frame]
            waves[pl.ds(frame + t * tile, tile), lanes] = block[:, frame:]

    def correct(begin, count):
        lanes = pl.ds(begin * frame, count * frame)
        wave = times_left(tables[0], tables[1], waves[:, lanes])
        real, imag = wave[:frame], wave[frame:]
        factor = amplitude[:, lanes] * jnp.minimum(
            lax.rsqrt(real * real + imag * imag), 1.0 / MODULUS_FLOOR)
        waves[:, lanes] = times_left(
            tables[2], tables[3], jnp.concatenate([real * factor, imag * factor], axis=0))

    def backward_rows(t):
        cols = pl.ds(t * tile, tile)
        stacked = []
        for j in range(frames):
            lanes = pl.ds(j * frame, frame)
            stacked.append(jnp.concatenate(
                [waves[cols, lanes], waves[pl.ds(frame + t * tile, tile), lanes]], axis=1))
        out = times_right(jnp.concatenate(stacked, axis=0), tables[0], tables[1])
        back_real, back_imag = [], []
        for j in range(frames):
            block = out[j * tile : (j + 1) * tile]
            real, imag = block[:, :frame], block[:, frame:]
            p_real, p_imag = rolled[j, 0, cols, :], rolled[j, 1, cols, :]
            back_real.append(p_real * real + p_imag * imag)
            back_imag.append(p_real * imag - p_imag * real)
        for channel, pieces in enumerate((back_real, back_imag)):
            for target, value in unfold(t, pieces):
                summed[channel, pl.ds(target * tile, tile), :] = value

    order = sorted(range(1, bands - 1), key=lambda t: -abs(t - reach))

    def iterate(iteration, carry):
        est_copy(OUT).start()
        est_copy(PAIR).start()
        forward_rows(reach)
        est_copy(OUT).wait_send()
        est_copy(FAR).start()
        est_copy(OUT).wait_recv()
        est_copy(EXTRA).start()
        est_copy(PAIR).wait()
        for t in order:
            if t != reach:
                forward_rows(t)
        est_copy(FAR).wait()
        est_copy(EXTRA).wait()

        @pl.when(iteration == 0)
        def _():
            for t in offsets:
                cover_copy(t).start()

        forward_rows(0)
        step = 2 if frames % 2 == 0 else 1
        for begin in range(0, frames, step):
            correct(begin, step)
        backward_rows(0)
        sum_copy(EXTRA).start()
        sum_copy(FAR).start()
        for t in order:
            if t != reach:
                backward_rows(t)
        sum_copy(PAIR).start()
        sum_copy(EXTRA).wait()
        for channel in range(2):
            summed[channel, tile_at(1), :] += sums_in[EXTRA, channel]
        sum_copy(OUT).start()
        backward_rows(reach)

        @pl.when(iteration == 0)
        def _():
            for t in offsets:
                cover_copy(t).wait()
            total = cover[mine, :]
            for t in offsets:
                total = total + cover_in[t]
            inverse[...] = 1.0 / (total + INTERSECTION_WEIGHT)

        for role in (PAIR, FAR, OUT):
            sum_copy(role).wait()
        for channel in range(2):
            total = summed[channel, mine, :]
            for role in (PAIR, FAR, OUT):
                total = total + sums_in[role, channel]
            old = source[channel, mine, :]
            source[channel, mine, :] = (total + INTERSECTION_WEIGHT * old) * inverse[...]
        return carry

    lax.fori_loop(0, ITERS, iterate, 0)

    for channel in range(2):
        gathered[ang, channel, pl.ds(SH, tile), :] = source[channel, mine, :] - first[channel]

    def edge_copy(side):
        begin, end = (SH, SH + tile) if side == 0 else (tile, 0)
        return pltpu.make_async_remote_copy(
            src_ref=gathered.at[ang, :, pl.ds(begin, SH), :], dst_ref=gathered.at[ang, :, pl.ds(end, SH), :],
            send_sem=edge_send.at[side], recv_sem=edge_recv.at[side],
            device_id={"pos": at(-1 if side == 0 else 1)}, device_id_type=MESH)

    def core_copy(d, slot):
        part = gathered.at[slot, :, pl.ds(SH, tile), :]
        return pltpu.make_async_remote_copy(
            src_ref=part, dst_ref=part, send_sem=core_send.at[d], recv_sem=core_recv.at[d],
            device_id={"ang": peer(d)}, device_id_type=MESH)

    def side_copy(d, side, slot):
        part = gathered.at[slot, :, pl.ds(0 if side == 0 else SH + tile, SH), :]
        return pltpu.make_async_remote_copy(
            src_ref=part, dst_ref=part, send_sem=side_send.at[d, side], recv_sem=side_recv.at[d, side],
            device_id={"ang": peer(d)}, device_id_type=MESH)

    for side in range(2):
        edge_copy(side).start()
    for d in range(1, n_ang):
        core_copy(d, ang).start()
    for side in range(2):
        edge_copy(side).wait()
    for d in range(1, n_ang):
        for side in range(2):
            side_copy(d, side, ang).start()
    for d in range(1, n_ang):
        core_copy(d, ang).wait_send()
        core_copy(d, peer(-d)).wait_recv()
        for side in range(2):
            side_copy(d, side, ang).wait_send()
            side_copy(d, side, peer(-d)).wait_recv()


def spread_kernel(weight, steps, object_block, gathered, out):
    _, depth, tile, rows = object_block.shape
    n_ang, _, wide, _ = gathered.shape
    first_layer = pl.program_id(0) * depth
    lane = lax.broadcasted_iota(jnp.int32, (tile, n_ang * wide), 1)
    offset = lane - lax.broadcasted_iota(jnp.int32, (tile, n_ang * wide), 0)
    blocks = []
    for z in range(depth):
        chosen = None
        for a in range(n_ang):
            begin = a * wide
            inside = (lane >= begin) & (lane < begin + wide)
            hit = inside & (offset == begin + SH - steps[a, first_layer + z])
            chosen = hit if chosen is None else chosen | hit
        blocks.append(jnp.where(chosen, 1.0, 0.0))
    pick = jnp.concatenate(blocks, axis=0).astype(BF16)
    for channel in range(2):
        high, low = split(gathered[:, channel].reshape(n_ang * wide, rows))
        total = dot(pick, high) + dot(pick, low)
        out[channel] = object_block[channel] + weight * total.reshape(depth, tile, rows)


def per_device(n_pos, n_ang, object_field, probe_wave, intensity, positions, shear_steps):
    _, layers, tile, rows = object_field.shape
    frame = probe_wave.shape[1]
    frames = positions.shape[0]
    reach = -(-(frame // 2) // tile)
    bands = 2 * reach + 1
    assert intensity.shape[0] == 1 and frame == 2 * reach * tile and rows == 2 * frame
    assert n_pos >= bands and n_pos % 2 == 0 and reach == 2
    tables = jnp.asarray(dft_tables(frame))
    wide = tile + 2 * SH
    vmem = pl.BlockSpec(memory_space=pltpu.VMEM)
    smem = pl.BlockSpec(memory_space=pltpu.SMEM)
    dma = pltpu.SemaphoreType.DMA
    gathered = pl.pallas_call(
        functools.partial(update_kernel, n_pos, n_ang),
        out_shape=jax.ShapeDtypeStruct((n_ang, 2, wide, rows), F32),
        in_specs=[smem, smem, pl.BlockSpec(memory_space=pl.ANY), vmem, vmem, vmem],
        out_specs=vmem,
        scratch_shapes=[
            pltpu.VMEM((2, layers, tile, rows), F32),
            pltpu.VMEM((frames, 2, frame, frame), F32),
            pltpu.VMEM((frame, frames * frame), F32),
            pltpu.VMEM((bands * tile, rows), F32),
            pltpu.VMEM((bands, tile, rows), F32),
            pltpu.VMEM((tile, rows), F32),
            pltpu.VMEM((2, wide, rows), F32),
            pltpu.VMEM((2, 2, SH, rows), F32),
            pltpu.VMEM((2, tile, rows), F32),
            pltpu.VMEM((2, bands * tile, rows), F32),
            pltpu.VMEM((2, bands * tile, rows), F32),
            pltpu.VMEM((4, 2, tile, rows), F32),
            pltpu.VMEM((2 * frame, frames * frame), F32),
            dma,
            dma((bands,)), dma((bands,)), dma((2,)), dma((2,)), dma((4,)), dma((4,)),
            dma((4,)), dma((4,)), dma((2,)), dma((2,)), dma((n_ang,)), dma((n_ang,)),
            dma((n_ang, 2)), dma((n_ang, 2)),
        ],
        compiler_params=pltpu.CompilerParams(collective_id=0, has_side_effects=True),
        name="update",
    )(positions.T, shear_steps, object_field, probe_wave, intensity[0], tables)

    depth = 8 if layers % 8 == 0 else layers
    block = pl.BlockSpec((2, depth, tile, rows), lambda i: (0, i, 0, 0))
    return pl.pallas_call(
        functools.partial(spread_kernel, RELAXATION / shear_steps.shape[0]),
        out_shape=jax.ShapeDtypeStruct(object_field.shape, F32),
        grid=(layers // depth,),
        in_specs=[smem, block, vmem],
        out_specs=block,
        name="spread",
    )(shear_steps, object_field, gathered)


def solution(mesh):
    placed = (P(None, None, "pos", None), P(), P("ang", "pos", None, None), P("pos", None), P())
    return jax.shard_map(
        functools.partial(per_device, mesh.shape["pos"], mesh.shape["ang"]),
        mesh=mesh,
        in_specs=placed,
        out_specs=P(None, None, "pos", None),
        check_vma=False,
    )
```

```python
import functools

import jax
import jax.numpy as jnp
import numpy as np
from jax import lax
from jax.experimental import pallas as pl
from jax.experimental.pallas import tpu as pltpu
from jax.sharding import PartitionSpec as P

SH = 8
ITERS = 3
MODULUS_FLOOR = 0.25
INTERSECTION_WEIGHT = 1.0
RELAXATION = 0.5
MESH = pl.DeviceIdType.MESH
F32 = jnp.float32
BF16 = jnp.bfloat16
OUT, PAIR, FAR, EXTRA = range(4)


def dft_tables(length):
    index = np.arange(length)
    phases = (index[:, None] * index[None, :] % length) * (2.0 * np.pi / length)
    cosine = np.cos(phases) / np.sqrt(length)
    sine = np.sin(phases) / np.sqrt(length)
    a = np.block([[cosine, sine], [-sine, cosine]])
    parts = []
    for table in (a, a.T):
        high = table.astype(np.float32).astype(jnp.bfloat16)
        low = (table - high.astype(np.float64)).astype(np.float32).astype(jnp.bfloat16)
        parts += [high, low]
    return np.stack(parts)


def split(x):
    high = x.astype(BF16)
    return high, (x - high.astype(F32)).astype(BF16)


def dot(a, b):
    return jnp.dot(a, b, preferred_element_type=F32)


def times_right(x, high, low):
    x_high, x_low = split(x)
    return dot(x_high, high) + (dot(x_low, high) + dot(x_high, low))


def times_left(high, low, x):
    x_high, x_low = split(x)
    return dot(high, x_high) + (dot(high, x_low) + dot(low, x_high))


def update_kernel(
    n_pos, n_ang,
    positions, steps, object_hbm, probe, intensity, tables,
    gathered,
    held, rolled, amplitude, cover, cover_in, inverse, canvas, rim_in, first, source, summed, sums_in, waves,
    load_sem, cover_send, cover_recv, rim_send, rim_recv, est_send, est_recv,
    sum_send, sum_recv, edge_send, edge_recv, core_send, core_recv, side_send, side_recv,
):
    me = lax.axis_index("pos")
    ang = lax.axis_index("ang")
    layers, tile, rows = held.shape[1], first.shape[1], first.shape[2]
    frame = probe.shape[1]
    half = rows - frame
    frames = positions.shape[1]
    bands = source.shape[1] // tile
    reach = bands // 2
    width = n_pos * tile
    offsets = [t for t in range(bands) if t != reach]

    def at(shift):
        return lax.rem(me + (shift + n_pos), n_pos)

    def peer(shift):
        return lax.rem(ang + (shift + n_ang), n_ang)

    load = pltpu.make_async_copy(object_hbm, held, load_sem)
    load.start()

    barrier = pltpu.get_barrier_semaphore()
    for t in offsets:
        pl.semaphore_signal(barrier, inc=1, device_id={"pos": at(t - reach)}, device_id_type=MESH)
    for d in range(1, n_ang):
        pl.semaphore_signal(barrier, inc=1, device_id={"ang": peer(d)}, device_id_type=MESH)

    lane = lax.broadcasted_iota(jnp.int32, (tile, frame), 1)
    row = lax.broadcasted_iota(jnp.int32, (tile, frame), 0)
    col_at = []
    row_at = []
    for j in range(frames):
        col_at.append(lax.rem(positions[0, j] - me * tile + (reach * tile + width), width))
        row_at.append(positions[1, j])

    def unfold(t, pieces):
        sums = [[None, None], [None, None]] if t == 0 else [[None, None]]
        zero = jnp.zeros((tile, frame), F32)
        for j, piece in enumerate(pieces):
            low_half = lane >= row_at[j]
            parts = [jnp.where(low_half, piece, zero), jnp.where(low_half, zero, piece)]
            for lanes in range(2):
                values = [parts[lanes]]
                if t == 0:
                    low_cols = row >= col_at[j]
                    values = [jnp.where(low_cols, parts[lanes], zero), jnp.where(low_cols, zero, parts[lanes])]
                for place, value in enumerate(values):
                    old = sums[place][lanes]
                    sums[place][lanes] = value if old is None else old + value
        targets = [t, bands - 1] if t == 0 else [t]
        return [(target, jnp.concatenate(sums[place], axis=1)) for place, target in enumerate(targets)]

    wide = tile + 2 * SH
    per_block = frame // tile
    lane_wide = lax.broadcasted_iota(jnp.int32, (wide, frame), 1)
    source_col = lax.rem(lane_wide, tile)
    layer_in = lane_wide // tile
    target_col = lax.broadcasted_iota(jnp.int32, (wide, frame), 0) - SH
    blocks = []
    for begin in range(0, layers, per_block):
        shift = jnp.full((wide, frame), steps[ang, begin], jnp.int32)
        for k in range(1, per_block):
            shift = jnp.where(layer_in == k, steps[ang, begin + k], shift)
        blocks.append(jnp.where(source_col == target_col + shift, 1.0, 0.0).astype(BF16))
    pick = jnp.concatenate(blocks, axis=1)
    load.wait()
    for channel in range(2):
        high, low = split(held[channel].reshape(layers * tile, rows))
        canvas[channel] = dot(pick, high) + dot(pick, low)

    pl.semaphore_wait(barrier, len(offsets) + n_ang - 1)

    def rim_copy(side):
        begin = 0 if side == 0 else SH + tile
        return pltpu.make_async_remote_copy(
            src_ref=canvas.at[:, pl.ds(begin, SH), :], dst_ref=rim_in.at[side],
            send_sem=rim_send.at[side], recv_sem=rim_recv.at[side],
            device_id={"pos": at(-1 if side == 0 else 1)}, device_id_type=MESH)

    for side in range(2):
        rim_copy(side).start()
    for j in range(frames):
        for channel in range(2):
            value = pltpu.roll(probe[channel], col_at[j], 0)
            rolled[j, channel] = pltpu.roll(value, lax.rem(row_at[j], frame), 1)
        amplitude[:, pl.ds(j * frame, frame)] = jnp.sqrt(intensity[j])
    for t in range(bands - 1):
        cols = pl.ds(t * tile, tile)
        powers = [rolled[j, 0, cols, :] ** 2 + rolled[j, 1, cols, :] ** 2 for j in range(frames)]
        for target, value in unfold(t, powers):
            cover[pl.ds(target * tile, tile), :] = value

    def cover_copy(t):
        return pltpu.make_async_remote_copy(
            src_ref=cover.at[pl.ds(t * tile, tile), :], dst_ref=cover_in.at[t],
            send_sem=cover_send.at[t], recv_sem=cover_recv.at[t],
            device_id={"pos": at(t - reach)}, device_id_type=MESH)

    mine = pl.ds(reach * tile, tile)
    for side in range(2):
        rim_copy(side).wait()
    for channel in range(2):
        low = canvas[channel, pl.ds(SH, SH), :] + rim_in[1, channel]
        middle = canvas[channel, pl.ds(2 * SH, tile - 2 * SH), :]
        high = canvas[channel, pl.ds(tile, SH), :] + rim_in[0, channel]
        value = jnp.concatenate([low, middle, high], axis=0)
        first[channel] = value
        source[channel, mine, :] = value

    out_sign = 2 * lax.rem(me, 2) - 1

    def tile_at(step):
        return pl.ds(pl.multiple_of((reach + step * out_sign) * tile, tile), tile)

    def est_copy(role):
        sent, to, landing = (
            (0, 1, -1), (0, -1, 1), (0, -2, 2), (1, -1, 2))[role]
        return pltpu.make_async_remote_copy(
            src_ref=source.at[:, tile_at(sent), :], dst_ref=source.at[:, tile_at(landing), :],
            send_sem=est_send.at[role], recv_sem=est_recv.at[role],
            device_id={"pos": at(to * out_sign)}, device_id_type=MESH)

    def sum_copy(role):
        sent, to = ((1, 1), (-1, -1), (2, 2), (-2, -1))[role]
        return pltpu.make_async_remote_copy(
            src_ref=summed.at[:, tile_at(sent), :], dst_ref=sums_in.at[role],
            send_sem=sum_send.at[role], recv_sem=sum_recv.at[role],
            device_id={"pos": at(to * out_sign)}, device_id_type=MESH)

    def fold(t, channel, j):
        low_half = lane >= row_at[j]

        def columns(at_tile):
            cols = pl.ds(at_tile * tile, tile)
            return jnp.where(
                low_half, source[channel, cols, pl.ds(0, frame)], source[channel, cols, pl.ds(half, frame)])

        if t > 0:
            return columns(t)
        return jnp.where(row >= col_at[j], columns(0), columns(bands - 1))

    def forward_rows(t):
        cols = pl.ds(t * tile, tile)
        stacked = []
        for j in range(frames):
            real, imag = fold(t, 0, j), fold(t, 1, j)
            p_real, p_imag = rolled[j, 0, cols, :], rolled[j, 1, cols, :]
            stacked.append(jnp.concatenate(
                [p_real * real - p_imag * imag, p_real * imag + p_imag * real], axis=1))
        out = times_right(jnp.concatenate(stacked, axis=0), tables[2], tables[3])
        for j in range(frames):
            block = out[j * tile : (j + 1) * tile]
            lanes = pl.ds(j * frame, frame)
            waves[cols, lanes] = block[:, :frame]
            waves[pl.ds(frame + t * tile, tile), lanes] = block[:, frame:]

    def correct(begin, count):
        lanes = pl.ds(begin * frame, count * frame)
        wave = times_left(tables[0], tables[1], waves[:, lanes])
        real, imag = wave[:frame], wave[frame:]
        factor = amplitude[:, lanes] * jnp.minimum(
            lax.rsqrt(real * real + imag * imag), 1.0 / MODULUS_FLOOR)
        waves[:, lanes] = times_left(
            tables[2], tables[3], jnp.concatenate([real * factor, imag * factor], axis=0))

    def backward_rows(t):
        cols = pl.ds(t * tile, tile)
        stacked = []
        for j in range(frames):
            lanes = pl.ds(j * frame, frame)
            stacked.append(jnp.concatenate(
                [waves[cols, lanes], waves[pl.ds(frame + t * tile, tile), lanes]], axis=1))
        out = times_right(jnp.concatenate(stacked, axis=0), tables[0], tables[1])
        back_real, back_imag = [], []
        for j in range(frames):
            block = out[j * tile : (j + 1) * tile]
            real, imag = block[:, :frame], block[:, frame:]
            p_real, p_imag = rolled[j, 0, cols, :], rolled[j, 1, cols, :]
            back_real.append(p_real * real + p_imag * imag)
            back_imag.append(p_real * imag - p_imag * real)
        for channel, pieces in enumerate((back_real, back_imag)):
            for target, value in unfold(t, pieces):
                summed[channel, pl.ds(target * tile, tile), :] = value

    order = sorted(range(1, bands - 1), key=lambda t: -abs(t - reach))

    def iterate(iteration, carry):
        est_copy(OUT).start()
        est_copy(PAIR).start()
        forward_rows(reach)
        est_copy(OUT).wait_send()
        est_copy(FAR).start()
        est_copy(OUT).wait_recv()
        est_copy(EXTRA).start()
        est_copy(PAIR).wait()
        for t in order:
            if t != reach:
                forward_rows(t)
        est_copy(FAR).wait()
        est_copy(EXTRA).wait()

        @pl.when(iteration == 0)
        def _():
            for t in offsets:
                cover_copy(t).start()

        forward_rows(0)
        step = 2 if frames % 2 == 0 else 1
        for begin in range(0, frames, step):
            correct(begin, step)
        backward_rows(0)
        sum_copy(EXTRA).start()
        sum_copy(FAR).start()
        for t in order:
            if t != reach:
                backward_rows(t)
        sum_copy(PAIR).start()
        sum_copy(EXTRA).wait()
        for channel in range(2):
            summed[channel, tile_at(1), :] += sums_in[EXTRA, channel]
        sum_copy(OUT).start()
        backward_rows(reach)

        @pl.when(iteration == 0)
        def _():
            for t in offsets:
                cover_copy(t).wait()
            total = cover[mine, :]
            for t in offsets:
                total = total + cover_in[t]
            inverse[...] = 1.0 / (total + INTERSECTION_WEIGHT)

        for role in (PAIR, FAR, OUT):
            sum_copy(role).wait()
        for channel in range(2):
            total = summed[channel, mine, :]
            for role in (PAIR, FAR, OUT):
                total = total + sums_in[role, channel]
            old = source[channel, mine, :]
            source[channel, mine, :] = (total + INTERSECTION_WEIGHT * old) * inverse[...]
        return carry

    lax.fori_loop(0, ITERS, iterate, 0)

    for channel in range(2):
        gathered[ang, channel, pl.ds(SH, tile), :] = source[channel, mine, :] - first[channel]

    def edge_copy(side):
        begin, end = (SH, SH + tile) if side == 0 else (tile, 0)
        return pltpu.make_async_remote_copy(
            src_ref=gathered.at[ang, :, pl.ds(begin, SH), :], dst_ref=gathered.at[ang, :, pl.ds(end, SH), :],
            send_sem=edge_send.at[side], recv_sem=edge_recv.at[side],
            device_id={"pos": at(-1 if side == 0 else 1)}, device_id_type=MESH)

    def core_copy(d, slot):
        part = gathered.at[slot, :, pl.ds(SH, tile), :]
        return pltpu.make_async_remote_copy(
            src_ref=part, dst_ref=part, send_sem=core_send.at[d], recv_sem=core_recv.at[d],
            device_id={"ang": peer(d)}, device_id_type=MESH)

    def side_copy(d, side, slot):
        part = gathered.at[slot, :, pl.ds(0 if side == 0 else SH + tile, SH), :]
        return pltpu.make_async_remote_copy(
            src_ref=part, dst_ref=part, send_sem=side_send.at[d, side], recv_sem=side_recv.at[d, side],
            device_id={"ang": peer(d)}, device_id_type=MESH)

    for side in range(2):
        edge_copy(side).start()
    for d in sorted(range(1, n_ang), key=lambda d: -min(d, n_ang - d)):
        core_copy(d, ang).start()
    for side in range(2):
        edge_copy(side).wait()
    for d in range(1, n_ang):
        for side in range(2):
            side_copy(d, side, ang).start()
    for d in range(1, n_ang):
        core_copy(d, ang).wait_send()
        core_copy(d, peer(-d)).wait_recv()
        for side in range(2):
            side_copy(d, side, ang).wait_send()
            side_copy(d, side, peer(-d)).wait_recv()


def spread_kernel(weight, steps, object_block, gathered, out):
    _, depth, tile, rows = object_block.shape
    n_ang, _, wide, _ = gathered.shape
    first_layer = pl.program_id(0) * depth
    offset = lax.broadcasted_iota(jnp.int32, (tile, n_ang * wide), 1) - lax.broadcasted_iota(
        jnp.int32, (tile, n_ang * wide), 0)
    lane = lax.broadcasted_iota(jnp.int32, (1, n_ang * wide), 1)
    blocks = []
    for z in range(depth):
        target = jnp.full((1, n_ang * wide), SH - steps[0, first_layer + z], jnp.int32)
        for a in range(1, n_ang):
            target = jnp.where(lane >= a * wide, a * wide + SH - steps[a, first_layer + z], target)
        blocks.append(jnp.where(offset == target, 1.0, 0.0))
    pick = jnp.concatenate(blocks, axis=0).astype(BF16)
    for channel in range(2):
        high, low = split(gathered[:, channel].reshape(n_ang * wide, rows))
        total = dot(pick, high) + dot(pick, low)
        out[channel] = object_block[channel] + weight * total.reshape(depth, tile, rows)


def per_device(n_pos, n_ang, object_field, probe_wave, intensity, positions, shear_steps):
    _, layers, tile, rows = object_field.shape
    frame = probe_wave.shape[1]
    frames = positions.shape[0]
    reach = -(-(frame // 2) // tile)
    bands = 2 * reach + 1
    assert intensity.shape[0] == 1 and frame == 2 * reach * tile and rows == 2 * frame
    assert n_pos >= bands and n_pos % 2 == 0 and reach == 2
    tables = jnp.asarray(dft_tables(frame))
    wide = tile + 2 * SH
    vmem = pl.BlockSpec(memory_space=pltpu.VMEM)
    smem = pl.BlockSpec(memory_space=pltpu.SMEM)
    dma = pltpu.SemaphoreType.DMA
    gathered = pl.pallas_call(
        functools.partial(update_kernel, n_pos, n_ang),
        out_shape=jax.ShapeDtypeStruct((n_ang, 2, wide, rows), F32),
        in_specs=[smem, smem, pl.BlockSpec(memory_space=pl.ANY), vmem, vmem, vmem],
        out_specs=vmem,
        scratch_shapes=[
            pltpu.VMEM((2, layers, tile, rows), F32),
            pltpu.VMEM((frames, 2, frame, frame), F32),
            pltpu.VMEM((frame, frames * frame), F32),
            pltpu.VMEM((bands * tile, rows), F32),
            pltpu.VMEM((bands, tile, rows), F32),
            pltpu.VMEM((tile, rows), F32),
            pltpu.VMEM((2, wide, rows), F32),
            pltpu.VMEM((2, 2, SH, rows), F32),
            pltpu.VMEM((2, tile, rows), F32),
            pltpu.VMEM((2, bands * tile, rows), F32),
            pltpu.VMEM((2, bands * tile, rows), F32),
            pltpu.VMEM((4, 2, tile, rows), F32),
            pltpu.VMEM((2 * frame, frames * frame), F32),
            dma,
            dma((bands,)), dma((bands,)), dma((2,)), dma((2,)), dma((4,)), dma((4,)),
            dma((4,)), dma((4,)), dma((2,)), dma((2,)), dma((n_ang,)), dma((n_ang,)),
            dma((n_ang, 2)), dma((n_ang, 2)),
        ],
        compiler_params=pltpu.CompilerParams(collective_id=0, has_side_effects=True),
        name="update",
    )(positions.T, shear_steps, object_field, probe_wave, intensity[0], tables)

    depth = 8 if layers % 8 == 0 else layers
    block = pl.BlockSpec((2, depth, tile, rows), lambda i: (0, i, 0, 0))
    return pl.pallas_call(
        functools.partial(spread_kernel, RELAXATION / shear_steps.shape[0]),
        out_shape=jax.ShapeDtypeStruct(object_field.shape, F32),
        grid=(layers // depth,),
        in_specs=[smem, block, vmem],
        out_specs=block,
        name="spread",
    )(shear_steps, object_field, gathered)


def solution(mesh):
    placed = (P(None, None, "pos", None), P(), P("ang", "pos", None, None), P("pos", None), P())
    return jax.shard_map(
        functools.partial(per_device, mesh.shape["pos"], mesh.shape["ang"]),
        mesh=mesh,
        in_specs=placed,
        out_specs=P(None, None, "pos", None),
        check_vma=False,
    )
```

```python
import functools

import jax
import jax.numpy as jnp
import numpy as np
from jax import lax
from jax.experimental import pallas as pl
from jax.experimental.pallas import tpu as pltpu
from jax.sharding import PartitionSpec as P

SH = 8
ITERS = 3
MODULUS_FLOOR = 0.25
INTERSECTION_WEIGHT = 1.0
RELAXATION = 0.5
MESH = pl.DeviceIdType.MESH
F32 = jnp.float32
BF16 = jnp.bfloat16
OUT, PAIR, FAR, EXTRA = range(4)


def dft_tables(length):
    index = np.arange(length)
    phases = (index[:, None] * index[None, :] % length) * (2.0 * np.pi / length)
    cosine = np.cos(phases) / np.sqrt(length)
    sine = np.sin(phases) / np.sqrt(length)
    a = np.block([[cosine, sine], [-sine, cosine]])
    parts = []
    for table in (a, a.T):
        high = table.astype(np.float32).astype(jnp.bfloat16)
        low = (table - high.astype(np.float64)).astype(np.float32).astype(jnp.bfloat16)
        parts += [high, low]
    return np.stack(parts)


def split(x):
    high = x.astype(BF16)
    return high, (x - high.astype(F32)).astype(BF16)


def dot(a, b):
    return jnp.dot(a, b, preferred_element_type=F32)


def times_right(x, high, low):
    x_high, x_low = split(x)
    return dot(x_high, high) + (dot(x_low, high) + dot(x_high, low))


def times_left(high, low, x):
    x_high, x_low = split(x)
    return dot(high, x_high) + (dot(high, x_low) + dot(low, x_high))


def update_kernel(
    n_pos, n_ang,
    positions, steps, object_hbm, probe, intensity, tables,
    gathered,
    held, rolled, amplitude, cover, cover_in, inverse, canvas, rim_in, first, source, summed, sums_in, waves,
    load_sem, cover_send, cover_recv, rim_send, rim_recv, est_send, est_recv,
    sum_send, sum_recv, edge_send, edge_recv, core_send, core_recv, side_send, side_recv,
):
    me = lax.axis_index("pos")
    ang = lax.axis_index("ang")
    layers, tile, rows = held.shape[1], first.shape[1], first.shape[2]
    frame = probe.shape[1]
    half = rows - frame
    frames = positions.shape[1]
    bands = source.shape[1] // tile
    reach = bands // 2
    width = n_pos * tile
    offsets = [t for t in range(bands) if t != reach]

    def at(shift):
        return lax.rem(me + (shift + n_pos), n_pos)

    def peer(shift):
        return lax.rem(ang + (shift + n_ang), n_ang)

    load = pltpu.make_async_copy(object_hbm, held, load_sem)
    load.start()

    barrier = pltpu.get_barrier_semaphore()
    for t in offsets:
        pl.semaphore_signal(barrier, inc=1, device_id={"pos": at(t - reach)}, device_id_type=MESH)
    for d in range(1, n_ang):
        pl.semaphore_signal(barrier, inc=1, device_id={"ang": peer(d)}, device_id_type=MESH)

    lane = lax.broadcasted_iota(jnp.int32, (tile, frame), 1)
    row = lax.broadcasted_iota(jnp.int32, (tile, frame), 0)
    col_at = []
    row_at = []
    for j in range(frames):
        col_at.append(lax.rem(positions[0, j] - me * tile + (reach * tile + width), width))
        row_at.append(positions[1, j])

    def unfold(t, pieces):
        sums = [[None, None], [None, None]] if t == 0 else [[None, None]]
        zero = jnp.zeros((tile, frame), F32)
        for j, piece in enumerate(pieces):
            low_half = lane >= row_at[j]
            parts = [jnp.where(low_half, piece, zero), jnp.where(low_half, zero, piece)]
            for lanes in range(2):
                values = [parts[lanes]]
                if t == 0:
                    low_cols = row >= col_at[j]
                    values = [jnp.where(low_cols, parts[lanes], zero), jnp.where(low_cols, zero, parts[lanes])]
                for place, value in enumerate(values):
                    old = sums[place][lanes]
                    sums[place][lanes] = value if old is None else old + value
        targets = [t, bands - 1] if t == 0 else [t]
        return [(target, jnp.concatenate(sums[place], axis=1)) for place, target in enumerate(targets)]

    wide = tile + 2 * SH
    per_block = frame // tile
    lane_wide = lax.broadcasted_iota(jnp.int32, (wide, frame), 1)
    source_col = lax.rem(lane_wide, tile)
    layer_in = lane_wide // tile
    target_col = lax.broadcasted_iota(jnp.int32, (wide, frame), 0) - SH
    blocks = []
    for begin in range(0, layers, per_block):
        shift = jnp.full((wide, frame), steps[ang, begin], jnp.int32)
        for k in range(1, per_block):
            shift = jnp.where(layer_in == k, steps[ang, begin + k], shift)
        blocks.append(jnp.where(source_col == target_col + shift, 1.0, 0.0).astype(BF16))
    pick = jnp.concatenate(blocks, axis=1)
    load.wait()
    for channel in range(2):
        high, low = split(held[channel].reshape(layers * tile, rows))
        canvas[channel] = dot(pick, high) + dot(pick, low)

    pl.semaphore_wait(barrier, len(offsets) + n_ang - 1)

    def rim_copy(side):
        begin = 0 if side == 0 else SH + tile
        return pltpu.make_async_remote_copy(
            src_ref=canvas.at[:, pl.ds(begin, SH), :], dst_ref=rim_in.at[side],
            send_sem=rim_send.at[side], recv_sem=rim_recv.at[side],
            device_id={"pos": at(-1 if side == 0 else 1)}, device_id_type=MESH)

    for side in range(2):
        rim_copy(side).start()
    for j in range(frames):
        for channel in range(2):
            value = pltpu.roll(probe[channel], col_at[j], 0)
            rolled[j, channel] = pltpu.roll(value, lax.rem(row_at[j], frame), 1)
        amplitude[:, pl.ds(j * frame, frame)] = jnp.sqrt(intensity[j])
    for t in range(bands - 1):
        cols = pl.ds(t * tile, tile)
        powers = [rolled[j, 0, cols, :] ** 2 + rolled[j, 1, cols, :] ** 2 for j in range(frames)]
        for target, value in unfold(t, powers):
            cover[pl.ds(target * tile, tile), :] = value

    def cover_copy(t):
        return pltpu.make_async_remote_copy(
            src_ref=cover.at[pl.ds(t * tile, tile), :], dst_ref=cover_in.at[t],
            send_sem=cover_send.at[t], recv_sem=cover_recv.at[t],
            device_id={"pos": at(t - reach)}, device_id_type=MESH)

    mine = pl.ds(reach * tile, tile)
    for side in range(2):
        rim_copy(side).wait()
    for channel in range(2):
        low = canvas[channel, pl.ds(SH, SH), :] + rim_in[1, channel]
        middle = canvas[channel, pl.ds(2 * SH, tile - 2 * SH), :]
        high = canvas[channel, pl.ds(tile, SH), :] + rim_in[0, channel]
        value = jnp.concatenate([low, middle, high], axis=0)
        first[channel] = value
        source[channel, mine, :] = value

    out_sign = 2 * lax.rem(me, 2) - 1

    def tile_at(step):
        return pl.ds(pl.multiple_of((reach + step * out_sign) * tile, tile), tile)

    def est_copy(role):
        sent, to, landing = (
            (0, 1, -1), (0, -1, 1), (0, -2, 2), (1, -1, 2))[role]
        return pltpu.make_async_remote_copy(
            src_ref=source.at[:, tile_at(sent), :], dst_ref=source.at[:, tile_at(landing), :],
            send_sem=est_send.at[role], recv_sem=est_recv.at[role],
            device_id={"pos": at(to * out_sign)}, device_id_type=MESH)

    def sum_copy(role):
        sent, to = ((1, 1), (-1, -1), (2, 2), (-2, -1))[role]
        return pltpu.make_async_remote_copy(
            src_ref=summed.at[:, tile_at(sent), :], dst_ref=sums_in.at[role],
            send_sem=sum_send.at[role], recv_sem=sum_recv.at[role],
            device_id={"pos": at(to * out_sign)}, device_id_type=MESH)

    def fold(t, channel, j):
        low_half = lane >= row_at[j]

        def columns(at_tile):
            cols = pl.ds(at_tile * tile, tile)
            return jnp.where(
                low_half, source[channel, cols, pl.ds(0, frame)], source[channel, cols, pl.ds(half, frame)])

        if t > 0:
            return columns(t)
        return jnp.where(row >= col_at[j], columns(0), columns(bands - 1))

    def forward_rows(t):
        cols = pl.ds(t * tile, tile)
        stacked = []
        for j in range(frames):
            real, imag = fold(t, 0, j), fold(t, 1, j)
            p_real, p_imag = rolled[j, 0, cols, :], rolled[j, 1, cols, :]
            stacked.append(jnp.concatenate(
                [p_real * real - p_imag * imag, p_real * imag + p_imag * real], axis=1))
        out = times_right(jnp.concatenate(stacked, axis=0), tables[2], tables[3])
        for j in range(frames):
            block = out[j * tile : (j + 1) * tile]
            lanes = pl.ds(j * frame, frame)
            waves[cols, lanes] = block[:, :frame]
            waves[pl.ds(frame + t * tile, tile), lanes] = block[:, frame:]

    def correct(begin, count):
        lanes = pl.ds(begin * frame, count * frame)
        wave = times_left(tables[0], tables[1], waves[:, lanes])
        real, imag = wave[:frame], wave[frame:]
        factor = amplitude[:, lanes] * jnp.minimum(
            lax.rsqrt(real * real + imag * imag), 1.0 / MODULUS_FLOOR)
        waves[:, lanes] = times_left(
            tables[2], tables[3], jnp.concatenate([real * factor, imag * factor], axis=0))

    def backward_rows(t):
        cols = pl.ds(t * tile, tile)
        stacked = []
        for j in range(frames):
            lanes = pl.ds(j * frame, frame)
            stacked.append(jnp.concatenate(
                [waves[cols, lanes], waves[pl.ds(frame + t * tile, tile), lanes]], axis=1))
        out = times_right(jnp.concatenate(stacked, axis=0), tables[0], tables[1])
        back_real, back_imag = [], []
        for j in range(frames):
            block = out[j * tile : (j + 1) * tile]
            real, imag = block[:, :frame], block[:, frame:]
            p_real, p_imag = rolled[j, 0, cols, :], rolled[j, 1, cols, :]
            back_real.append(p_real * real + p_imag * imag)
            back_imag.append(p_real * imag - p_imag * real)
        for channel, pieces in enumerate((back_real, back_imag)):
            for target, value in unfold(t, pieces):
                summed[channel, pl.ds(target * tile, tile), :] = value

    order = sorted(range(1, bands - 1), key=lambda t: -abs(t - reach))

    def iterate(iteration, carry):
        est_copy(OUT).start()
        est_copy(PAIR).start()
        forward_rows(reach)
        est_copy(OUT).wait_send()
        est_copy(FAR).start()
        est_copy(OUT).wait_recv()
        est_copy(EXTRA).start()
        est_copy(PAIR).wait()
        for t in order:
            if t != reach:
                forward_rows(t)
        est_copy(FAR).wait()
        est_copy(EXTRA).wait()

        @pl.when(iteration == 0)
        def _():
            for t in offsets:
                cover_copy(t).start()

        forward_rows(0)
        step = 2 if frames % 2 == 0 else 1
        for begin in range(0, frames, step):
            correct(begin, step)
        backward_rows(0)
        sum_copy(EXTRA).start()
        sum_copy(FAR).start()
        for t in order:
            if t != reach:
                backward_rows(t)
        sum_copy(PAIR).start()
        sum_copy(EXTRA).wait()
        for channel in range(2):
            summed[channel, tile_at(1), :] += sums_in[EXTRA, channel]
        sum_copy(OUT).start()
        backward_rows(reach)

        @pl.when(iteration == 0)
        def _():
            for t in offsets:
                cover_copy(t).wait()
            total = cover[mine, :]
            for t in offsets:
                total = total + cover_in[t]
            inverse[...] = 1.0 / (total + INTERSECTION_WEIGHT)

        for role in (PAIR, FAR, OUT):
            sum_copy(role).wait()
        for channel in range(2):
            total = summed[channel, mine, :]
            for role in (PAIR, FAR, OUT):
                total = total + sums_in[role, channel]
            old = source[channel, mine, :]
            source[channel, mine, :] = (total + INTERSECTION_WEIGHT * old) * inverse[...]
        return carry

    lax.fori_loop(0, ITERS, iterate, 0)

    for channel in range(2):
        gathered[ang, channel, pl.ds(SH, tile), :] = source[channel, mine, :] - first[channel]

    def edge_copy(side):
        begin, end = (SH, SH + tile) if side == 0 else (tile, 0)
        return pltpu.make_async_remote_copy(
            src_ref=gathered.at[ang, :, pl.ds(begin, SH), :], dst_ref=gathered.at[ang, :, pl.ds(end, SH), :],
            send_sem=edge_send.at[side], recv_sem=edge_recv.at[side],
            device_id={"pos": at(-1 if side == 0 else 1)}, device_id_type=MESH)

    def core_copy(d, slot):
        part = gathered.at[slot, :, pl.ds(SH, tile), :]
        return pltpu.make_async_remote_copy(
            src_ref=part, dst_ref=part, send_sem=core_send.at[d], recv_sem=core_recv.at[d],
            device_id={"ang": peer(d)}, device_id_type=MESH)

    def side_copy(d, side, slot):
        part = gathered.at[slot, :, pl.ds(0 if side == 0 else SH + tile, SH), :]
        return pltpu.make_async_remote_copy(
            src_ref=part, dst_ref=part, send_sem=side_send.at[d, side], recv_sem=side_recv.at[d, side],
            device_id={"ang": peer(d)}, device_id_type=MESH)

    for side in range(2):
        edge_copy(side).start()
    for d in sorted(range(1, n_ang), key=lambda d: -min(d, n_ang - d)):
        core_copy(d, ang).start()
    for side in range(2):
        edge_copy(side).wait()
    for d in range(1, n_ang):
        for side in range(2):
            side_copy(d, side, ang).start()
    for d in range(1, n_ang):
        core_copy(d, ang).wait_send()
        core_copy(d, peer(-d)).wait_recv()
        for side in range(2):
            side_copy(d, side, ang).wait_send()
            side_copy(d, side, peer(-d)).wait_recv()


def spread_kernel(weight, steps, object_block, gathered, out):
    _, depth, tile, rows = object_block.shape
    n_ang, _, wide, _ = gathered.shape
    first_layer = pl.program_id(0) * depth
    offset = lax.broadcasted_iota(jnp.int32, (tile, n_ang * wide), 1) - lax.broadcasted_iota(
        jnp.int32, (tile, n_ang * wide), 0)
    lane = lax.broadcasted_iota(jnp.int32, (1, n_ang * wide), 1)
    blocks = []
    for z in range(depth):
        target = jnp.full((1, n_ang * wide), SH - steps[0, first_layer + z], jnp.int32)
        for a in range(1, n_ang):
            target = jnp.where(lane >= a * wide, a * wide + SH - steps[a, first_layer + z], target)
        blocks.append(jnp.where(offset == target, 1.0, 0.0))
    pick = jnp.concatenate(blocks, axis=0).astype(BF16)
    for channel in range(2):
        high, low = split(gathered[:, channel].reshape(n_ang * wide, rows))
        total = dot(pick, high) + dot(pick, low)
        out[channel] = object_block[channel] + weight * total.reshape(depth, tile, rows)


def per_device(n_pos, n_ang, object_field, probe_wave, intensity, positions, shear_steps):
    _, layers, tile, rows = object_field.shape
    frame = probe_wave.shape[1]
    frames = positions.shape[0]
    reach = -(-(frame // 2) // tile)
    bands = 2 * reach + 1
    assert intensity.shape[0] == 1 and frame == 2 * reach * tile and rows == 2 * frame
    assert n_pos >= bands and n_pos % 2 == 0 and reach == 2
    tables = jnp.asarray(dft_tables(frame))
    wide = tile + 2 * SH
    vmem = pl.BlockSpec(memory_space=pltpu.VMEM)
    smem = pl.BlockSpec(memory_space=pltpu.SMEM)
    dma = pltpu.SemaphoreType.DMA
    gathered = pl.pallas_call(
        functools.partial(update_kernel, n_pos, n_ang),
        out_shape=jax.ShapeDtypeStruct((n_ang, 2, wide, rows), F32),
        in_specs=[smem, smem, pl.BlockSpec(memory_space=pl.ANY), vmem, vmem, vmem],
        out_specs=vmem,
        scratch_shapes=[
            pltpu.VMEM((2, layers, tile, rows), F32),
            pltpu.VMEM((frames, 2, frame, frame), F32),
            pltpu.VMEM((frame, frames * frame), F32),
            pltpu.VMEM((bands * tile, rows), F32),
            pltpu.VMEM((bands, tile, rows), F32),
            pltpu.VMEM((tile, rows), F32),
            pltpu.VMEM((2, wide, rows), F32),
            pltpu.VMEM((2, 2, SH, rows), F32),
            pltpu.VMEM((2, tile, rows), F32),
            pltpu.VMEM((2, bands * tile, rows), F32),
            pltpu.VMEM((2, bands * tile, rows), F32),
            pltpu.VMEM((4, 2, tile, rows), F32),
            pltpu.VMEM((2 * frame, frames * frame), F32),
            dma,
            dma((bands,)), dma((bands,)), dma((2,)), dma((2,)), dma((4,)), dma((4,)),
            dma((4,)), dma((4,)), dma((2,)), dma((2,)), dma((n_ang,)), dma((n_ang,)),
            dma((n_ang, 2)), dma((n_ang, 2)),
        ],
        compiler_params=pltpu.CompilerParams(collective_id=0, has_side_effects=True),
        name="update",
    )(positions.T, shear_steps, object_field, probe_wave, intensity[0], tables)

    depth = 16 if layers % 16 == 0 else layers
    block = pl.BlockSpec((2, depth, tile, rows), lambda i: (0, i, 0, 0))
    return pl.pallas_call(
        functools.partial(spread_kernel, RELAXATION / shear_steps.shape[0]),
        out_shape=jax.ShapeDtypeStruct(object_field.shape, F32),
        grid=(layers // depth,),
        in_specs=[smem, block, vmem],
        out_specs=block,
        name="spread",
    )(shear_steps, object_field, gathered)


def solution(mesh):
    placed = (P(None, None, "pos", None), P(), P("ang", "pos", None, None), P("pos", None), P())
    return jax.shard_map(
        functools.partial(per_device, mesh.shape["pos"], mesh.shape["ang"]),
        mesh=mesh,
        in_specs=placed,
        out_specs=P(None, None, "pos", None),
        check_vma=False,
    )
```
